32 devices in a mesh: grp: 2 (over x), seq: 16 (over z, y, core).
Axes of the slice: x: 2, y: 2, z: 4, core: 2. Of those that a mesh axis runs over, the one named last changes fastest.
Arguments:
- hidden_in: bfloat16 [2048, 2048], P(('grp', 'seq')), parts along dimension 0, may hold values from -6 to 6
- queries: bfloat16 [2048, 2048], P(('grp', 'seq')), parts along dimension 0
- key_rows: bfloat16 [2048, 256], P(('grp', 'seq')), parts along dimension 0
- value_rows: bfloat16 [2048, 256], P(('grp', 'seq')), parts along dimension 0, may hold values from -6 to 6
- window_start: int32 [2048], P(('grp', 'seq')), parts along dimension 0, may hold values from 0 to 1023, as said below
- output_weight: bfloat16 [2048, 2048], P('seq'), may hold values from -0.125 to 0.125
- norm_gain: float32 [2048], replicated, may hold values from 0.25 to 1.75
- expert_ids: int32 [2048, 8], P(('grp', 'seq')), parts along dimension 0, may hold values from 0 to 15, all different within a row; in each aligned block of 64 rows (0 to 63, 64 to 127, ...) at most 48 rows name the same one
- route_weights: float32 [2048, 8], P(('grp', 'seq')), parts along dimension 0, may hold values from 0.05 to 0.5
- gate_weight: bfloat16 [16, 2048, 768], P('seq'), may hold values from -0.125 to 0.125
- up_weight: bfloat16 [16, 2048, 768], P('seq'), may hold values from -0.125 to 0.125
- down_weight: bfloat16 [16, 768, 2048], P('seq'), may hold values from -0.21875 to 0.21875
Outputs:
- layer_output: bfloat16 [2048, 2048], P(('grp', 'seq')), parts along dimension 0
The draws below stay inside these ranges and needn't reach their ends.
There are 2 independent parts, one for each index of `grp`. The reference program is written for one: setup_inputs(seed, part) draws one part's arguments, and reference() takes and returns one part's arrays. A program takes and returns all parts, laid end to end along the dimension named above; an argument that names none is the same for every part. Nothing has to cross between parts.
Inputs may be any that keep to these rules, and one draw needn't show every extreme that they name: window_start[p] <= p and window_start never falls along p; window_start[0] = 0; the last position starts a new document. `expert_ids`: each token names 8 different experts; among the 64 tokens of one device no expert is named by more than 48 tokens.
All inputs are finite; a program needn't handle non-finite values.
Results may differ from the reference program's by a relative error of at most 0.012.
Values may be sent and summed in bfloat16 or wider, within the bound.
No kernel may reach another device: no remote copies, remote signals or barrier semaphores. Data moves between devices by JAX's collectives and lax.ppermute only.
A program may use at most 128 MiB of HBM per device.

```python
import math
import jax
import jax.numpy as jnp
import numpy as np
from jax import lax

D = 2048
FF = 768
HEADS = 16
KV_HEADS = 2
HEAD_DIM = 128
TOP = 8
TOK_DEV = 64
TOKENS = 1024
EXPERTS = 16
MOST = 48
N_SEQ = 16


def shared_keys(key):
    base = jax.random.normal(jax.random.fold_in(key, 701), (TOKENS, KV_HEADS * HEAD_DIM), jnp.float32)
    return jnp.clip(base, -6.0, 6.0)


def draw_key_rows(key, part):
    return shared_keys(key).astype(jnp.bfloat16)


def draw_queries(key, part):
    result = jax.random.normal(jax.random.fold_in(key, 703), (TOKENS, HEADS * HEAD_DIM), jnp.float32)
    result = 3.0 * jnp.clip(result, -6.0, 6.0)
    return result.astype(jnp.bfloat16)


def draw_window_start(key, part):
    cuts = jax.random.randint(jax.random.fold_in(key, 704), (2,), 3 * TOKENS // 4, TOKENS)
    marks = jnp.zeros((TOKENS,), jnp.int32).at[cuts].set(1).at[TOKENS - 1].set(1)
    position = jnp.arange(TOKENS, dtype=jnp.int32)
    return lax.cummax(jnp.where(marks > 0, position, 0), axis=0).astype(jnp.int32)


def levels(stream_key, dims, cuts, least, largest):
    level = 1.0
    for dim, parts in cuts:
        heights = jax.random.uniform(jax.random.fold_in(jax.random.fold_in(stream_key, 6), dim), (parts,), jnp.float32, least / len(cuts), largest / len(cuts))
        level = level * jnp.repeat(jnp.exp(heights), dims[dim] // parts).reshape((-1,) + (1,) * (len(dims) - 1 - dim))
    return level


def deal_out(own_key, own, number, rows, number_of, top, bound, lean):
    order = jax.random.permutation(own_key, number_of)
    heavy_load, common = shares(number_of, rows * top, bound, lean, True), shares(number_of, rows * top, bound, lean, False)
    places = jnp.arange(number_of)

    def named(lengths, offset_by):
        used = int((lengths > 0).sum())
        fixed = max(1, used // 4)
        moved = fixed + (places - fixed + offset_by * (used - fixed)) % max(1, number_of - fixed)
        return jnp.zeros((number_of,), jnp.int32).at[order[jnp.where(places < fixed, places, moved)]].set(jnp.asarray(lengths, jnp.int32))

    lengths = jnp.where(number % 4 == 0, named(heavy_load, number // 4), named(common, number - number // 4 - 1))
    mixed = jax.random.permutation(jax.random.fold_in(own, 3), number_of)
    donor, taker = mixed[0:number_of // 2 * 2:2], mixed[1:number_of // 2 * 2:2]
    room = jnp.minimum(lengths[donor] - 1, bound - lengths[taker]) // 2
    room = jnp.where((donor == order[0]) | (taker == order[0]) | (lengths[taker] == 0), 0, jnp.maximum(room, 0))
    moved = jax.random.randint(jax.random.fold_in(own, 4), (number_of // 2,), 0, 1 << 20) % (room + 1)
    lengths = lengths.at[donor].add(-moved).at[taker].add(moved)
    members = jnp.searchsorted(jnp.cumsum(lengths), jnp.arange(rows * top), side="right").astype(jnp.int32)
    listing = members.reshape(top, rows).T
    listing = listing[jax.random.permutation(jax.random.fold_in(own, 1), rows)]
    offset_by = jax.random.randint(jax.random.fold_in(own, 2), (rows, 1), 0, top)
    return jnp.take_along_axis(listing, (jnp.arange(top)[None, :] + offset_by) % top, axis=1)


def shares(amount, total, reach, slope, full):
    weights = [(1 << 20) // math.isqrt(rank ** slope) + 1 for rank in range(1, amount + 1)]
    largest = reach if full else min(reach, max(-(-total // amount), total * weights[0] // sum(weights)))
    least = 1 if total - largest >= amount - 1 else 0
    given, spare = [largest] + [least] * (amount - 1), total - largest - least * (amount - 1)
    while spare > 0:
        candidates = [i for i in range(1, amount) if given[i] < largest] or [i for i in range(1, amount) if given[i] < reach]
        pool, left = sum([weights[i] for i in candidates]), spare
        for i in candidates:
            addition = min(reach - given[i], max(1, left * weights[i] // pool), spare)
            given[i] = given[i] + addition
            spare = spare - addition
    return np.array(given)


def scatter_about(own_key, extent, width, bound, shards=(), kind=jnp.bfloat16):
    gain = levels(own_key, extent, shards, -0.22, 0.18) if shards else 1.0
    drawn = jax.random.normal(own_key, extent, jnp.float32) * width * gain
    return jnp.minimum(jnp.maximum(drawn, -bound), bound).astype(kind)


def setup_inputs(seed: int = 0, part: int = 0) -> dict:
    seeds = jax.random.split(jax.random.key(seed), 13)
    part_keys = jax.random.split(jax.random.fold_in(seeds[12], part), 13)
    hidden_in = scatter_about(part_keys[0], (TOKENS, D), 1.0, 6.0, ((0, 16),))
    queries = draw_queries(jax.random.fold_in(jax.random.fold_in(seeds[12], part), 71), part)
    key_rows = draw_key_rows(jax.random.fold_in(jax.random.fold_in(seeds[12], part), 71), part)
    value_rows = scatter_about(part_keys[3], (TOKENS, KV_HEADS * HEAD_DIM), 1.0, 6.0, ((0, 16),))
    window_start = draw_window_start(jax.random.fold_in(jax.random.fold_in(seeds[12], part), 71), part)
    output_weight = scatter_about(seeds[5], (HEADS * HEAD_DIM, D), (HEADS * HEAD_DIM) ** -0.5, 0.125, ((0, 16),))
    norm_gain = jnp.clip(1.0 + 0.15 * jax.random.normal(seeds[6], (D,), jnp.float32), 0.25, 1.75)
    expert_ids_keys = jax.random.split(jax.random.fold_in(part_keys[7], 1), TOKENS // TOK_DEV)
    expert_ids_turns = jax.random.permutation(jax.random.fold_in(part_keys[7], 3), TOKENS // TOK_DEV)
    expert_ids = jax.vmap(lambda own, number: deal_out(jax.random.fold_in(part_keys[7], 2), own, number, TOK_DEV, EXPERTS, TOP, MOST, 2))(expert_ids_keys, expert_ids_turns).reshape((TOKENS, TOP))
    route_weights = jnp.clip(jnp.exp(math.log(0.5) - 2.3025851 * jax.random.uniform(part_keys[8], (TOKENS, TOP), jnp.float32) ** levels(part_keys[8], (TOKENS, TOP), ((0, 16),), -0.2, 0.2)), 0.05, 0.5)
    gate_weight = scatter_about(seeds[9], (EXPERTS, D, FF), D ** -0.5, 0.125, ((0, 16),))
    up_weight = scatter_about(seeds[10], (EXPERTS, D, FF), D ** -0.5, 0.125, ((0, 16),))
    down_weight = scatter_about(seeds[11], (EXPERTS, FF, D), FF ** -0.5, 0.21875, ((0, 16),))
    return {"hidden_in": hidden_in, "queries": queries, "key_rows": key_rows, "value_rows": value_rows, "window_start": window_start, "output_weight": output_weight, "norm_gain": norm_gain, "expert_ids": expert_ids, "route_weights": route_weights, "gate_weight": gate_weight, "up_weight": up_weight, "down_weight": down_weight}


def reference(hidden_in, queries, key_rows, value_rows, window_start, output_weight, norm_gain, expert_ids, route_weights, gate_weight, up_weight, down_weight):
    group_size = HEADS // KV_HEADS
    query_all = queries.astype(jnp.float32).reshape(TOKENS, KV_HEADS, group_size, HEAD_DIM)
    key_all = key_rows.astype(jnp.float32).reshape(TOKENS, KV_HEADS, HEAD_DIM)
    value_all = value_rows.astype(jnp.float32).reshape(TOKENS, KV_HEADS, HEAD_DIM)
    score_scale = HEAD_DIM ** (-0.5)
    key_pos = jnp.arange(TOKENS, dtype=jnp.int32)
    query_size = math.gcd(TOKENS, 512)

    def attend_rows(block_index):
        first = (block_index * query_size).astype(jnp.int32)
        query_part = lax.dynamic_slice_in_dim(query_all, first, query_size, 0)
        starts = lax.dynamic_slice_in_dim(window_start, first, query_size, 0)
        query_pos = first + jnp.arange(query_size, dtype=jnp.int32)
        scores = jnp.einsum('qkgd,nkd->kgqn', query_part, key_all, precision=lax.Precision.HIGHEST) * score_scale
        allowed = (key_pos[None, :] <= query_pos[:, None]) & (key_pos[None, :] >= starts[:, None])
        scores = jnp.where(allowed[None, None], scores, -1e+30)
        row_max = lax.optimization_barrier(jnp.max(scores, axis=-1))
        expo = jnp.where(allowed[None, None], jnp.exp(scores - row_max[..., None]), 0.0)
        denominator = lax.optimization_barrier(jnp.sum(expo, axis=-1))
        probs = lax.optimization_barrier(expo.astype(jnp.bfloat16)).astype(jnp.float32)
        summed = jnp.einsum('kgqn,nkd->kgqd', probs, value_all, precision=lax.Precision.HIGHEST)
        result = summed / denominator[..., None]
        return result.transpose(2, 0, 1, 3).reshape(query_size, HEADS * HEAD_DIM).astype(jnp.bfloat16)
    attended = lax.map(attend_rows, jnp.arange(TOKENS // query_size, dtype=jnp.int32)).reshape(TOKENS, HEADS * HEAD_DIM)
    projected = jnp.dot(attended, output_weight, preferred_element_type=jnp.float32)
    residual = (hidden_in.astype(jnp.float32) + projected).astype(jnp.bfloat16)
    resid_float = residual.astype(jnp.float32)
    normed = (resid_float * lax.rsqrt(lax.optimization_barrier(jnp.mean(resid_float * resid_float, axis=-1, keepdims=True)) + 1e-06) * norm_gain).astype(jnp.bfloat16)
    slot_ids = expert_ids.reshape(N_SEQ, TOK_DEV * TOP)
    onehot = (slot_ids[..., None] == jnp.arange(EXPERTS, dtype=jnp.int32)[None, None, :]).astype(jnp.int32)
    slot_rank = lax.optimization_barrier(jnp.sum((jnp.cumsum(onehot, axis=1) - 1) * onehot, axis=-1))
    source_dev = jnp.arange(N_SEQ, dtype=jnp.int32)[:, None]
    destination = ((slot_ids * N_SEQ + source_dev) * MOST + slot_rank).reshape(-1).astype(jnp.int32)
    slot_rows = jnp.repeat(normed, TOP, axis=0)
    buffer_rows = jnp.zeros((EXPERTS * N_SEQ * MOST, D), jnp.bfloat16).at[destination].set(slot_rows)
    per_expert = N_SEQ * MOST

    def run_expert(expert_index):
        inputs = lax.dynamic_slice_in_dim(buffer_rows, (expert_index * per_expert).astype(jnp.int32), per_expert, 0)
        gate_out = jnp.dot(inputs, gate_weight[expert_index], preferred_element_type=jnp.float32)
        up_out = jnp.dot(inputs, up_weight[expert_index], preferred_element_type=jnp.float32)
        inner = (jax.nn.silu(gate_out) * up_out).astype(jnp.bfloat16)
        return jnp.dot(inner, down_weight[expert_index], preferred_element_type=jnp.float32).astype(jnp.bfloat16)
    expert_out = lax.map(run_expert, jnp.arange(EXPERTS, dtype=jnp.int32)).reshape(-1, D)
    gathered = expert_out[destination].astype(jnp.float32).reshape(TOKENS, TOP, D)
    mixture = lax.optimization_barrier(jnp.sum(gathered * route_weights[..., None], axis=1))
    return (resid_float + mixture).astype(jnp.bfloat16)
```

```python
import jax
import jax.numpy as jnp
from jax import lax
from jax.sharding import PartitionSpec as P

HEADS = 16
KV_HEADS = 2
CHUNKS = 1


def spread_out(
    hidden_in,
    queries,
    key_rows,
    value_rows,
    window_start,
    output_weight,
    norm_gain,
    expert_ids,
    route_weights,
    gate_weight,
    up_weight,
    down_weight,
):
    tok_count = queries.shape[0]
    width_d = hidden_in.shape[1]
    head_dim = key_rows.shape[1] // KV_HEADS
    group_size = HEADS // KV_HEADS
    score_scale = head_dim ** (-0.5)
    device = lax.axis_index("seq")
    first_pos = device * tok_count
    query_pos = first_pos + jnp.arange(tok_count, dtype=jnp.int32)
    last_pos = first_pos + tok_count - 1
    first_start = window_start[0]
    query_block = (
        queries.reshape(tok_count, KV_HEADS, group_size, head_dim)
        .transpose(1, 2, 0, 3)
        .reshape(KV_HEADS, group_size * tok_count, head_dim)
    )
    query_rows = group_size * tok_count

    def attend(running, key_block, value_block, block_start):
        row_max, denominator, accumulated = running
        scores = (
            jnp.einsum("kmd,nkd->kmn", query_block, key_block, preferred_element_type=jnp.float32)
            * score_scale
        )
        key_pos = block_start + jnp.arange(key_block.shape[0], dtype=jnp.int32)
        allowed = (key_pos[None, :] <= query_pos[:, None]) & (
            key_pos[None, :] >= window_start[:, None]
        )
        allowed = jnp.tile(allowed, (group_size, 1))[None]
        scores = jnp.where(allowed, scores, -1e30)
        newest = jnp.maximum(row_max, jnp.max(scores, axis=-1))
        factor = jnp.exp(row_max - newest)
        weights = jnp.where(allowed, jnp.exp(scores - newest[..., None]), 0.0)
        denominator = denominator * factor + jnp.sum(weights, axis=-1)
        accumulated = accumulated * factor[..., None] + jnp.einsum(
            "kmn,nkd->kmd",
            weights.astype(jnp.bfloat16),
            value_block,
            preferred_element_type=jnp.float32,
        )
        return (newest, denominator, accumulated)

    initial = (
        jnp.full((KV_HEADS, query_rows), -1e30, jnp.float32),
        jnp.zeros((KV_HEADS, query_rows), jnp.float32),
        jnp.zeros((KV_HEADS, query_rows, head_dim), jnp.float32),
    )
    running = initial
    key_piece = lax.all_gather(key_rows, "seq", axis=0, tiled=True)
    value_piece = lax.all_gather(value_rows, "seq", axis=0, tiled=True)
    row_count = key_piece.shape[0]
    block_size = 512
    block_count = row_count // block_size
    key_blocks = key_piece.reshape(block_count, block_size, KV_HEADS, head_dim)
    value_blocks = value_piece.reshape(block_count, block_size, KV_HEADS, head_dim)

    def one_block(carried, block_index):
        block_start = block_index * block_size
        needed = (block_start <= last_pos) & (block_start + block_size - 1 >= first_start)
        carried = lax.cond(
            needed,
            lambda inner_state: attend(
                inner_state, key_blocks[block_index], value_blocks[block_index], block_start
            ),
            lambda inner_state: inner_state,
            carried,
        )
        return (carried, None)

    running, unused = lax.scan(one_block, running, jnp.arange(block_count, dtype=jnp.int32))
    row_max, denominator, accumulated = running
    attended = (
        (accumulated / denominator[..., None])
        .reshape(KV_HEADS, group_size, tok_count, head_dim)
        .transpose(2, 0, 1, 3)
        .reshape(tok_count, HEADS * head_dim)
        .astype(jnp.bfloat16)
    )
    projected = jnp.dot(
        attended,
        lax.all_gather(output_weight, "seq", axis=0, tiled=True),
        preferred_element_type=jnp.float32,
    )
    residual = (hidden_in.astype(jnp.float32) + projected).astype(jnp.bfloat16)
    resid_float = residual.astype(jnp.float32)
    normed = (
        resid_float
        * lax.rsqrt(jnp.mean(resid_float * resid_float, axis=-1, keepdims=True) + 1e-06)
        * norm_gain
    ).astype(jnp.bfloat16)
    top_count = expert_ids.shape[1]
    local_experts = gate_weight.shape[0]
    devices = lax.axis_size("seq")
    experts_all = devices * local_experts
    capacity = max(2, 3 * tok_count * top_count // (2 * experts_all))
    flat_ids = expert_ids.reshape(-1)
    onehot = (flat_ids[:, None] == jnp.arange(experts_all, dtype=jnp.int32)[None, :]).astype(
        jnp.int32
    )
    slot_rank = jnp.sum((jnp.cumsum(onehot, axis=0) - 1) * onehot, axis=1)
    destination = flat_ids * capacity + slot_rank
    slot_rows = jnp.repeat(normed, top_count, axis=0)
    outgoing = (
        jnp.zeros((experts_all * capacity, width_d), jnp.bfloat16).at[destination].set(slot_rows)
    )
    outgoing = outgoing.reshape(devices, local_experts, capacity, width_d)
    arrived = lax.all_to_all(outgoing, "seq", split_axis=0, concat_axis=0, tiled=True)
    inputs = arrived[:, 0].reshape(-1, width_d)
    gate_out = jnp.dot(inputs, gate_weight[0], preferred_element_type=jnp.float32)
    up_out = jnp.dot(inputs, up_weight[0], preferred_element_type=jnp.float32)
    inner = (jax.nn.silu(gate_out) * up_out).astype(jnp.bfloat16)
    result = jnp.dot(inner, down_weight[0], preferred_element_type=jnp.float32).astype(jnp.bfloat16)
    outputs = [result.reshape(arrived.shape[0], arrived.shape[2], width_d)]
    computed = jnp.stack(outputs, axis=1)
    returned = lax.all_to_all(computed, "seq", split_axis=0, concat_axis=0, tiled=True)
    gathered = (
        returned.reshape(experts_all * capacity, width_d)[destination]
        .astype(jnp.float32)
        .reshape(tok_count, top_count, width_d)
    )
    mixture = jnp.sum(gathered * route_weights[..., None], axis=1)
    return (resid_float + mixture).astype(jnp.bfloat16)


def swap(value, perm):
    return lax.ppermute(value, "seq", perm)


def permutations(size):
    ring = size // 4
    up = [(i, (i + 4) % size) for i in range(size)]
    down = [(i, (i - 4) % size) for i in range(size)]
    across = [(i, i ^ 2) for i in range(size)]
    core = [(i, i ^ 1) for i in range(size)]
    return ring, up, down, across, core


def gather_ring(value, size):
    ring, up, down, across, core = permutations(size)
    half = value.shape[0] // 2
    found = [None] * ring
    found[0] = value
    above = below = value
    for step in range(1, (ring + 1) // 2):
        above, below = swap(above, down), swap(below, up)
        found[step], found[ring - step] = above, below
    if ring % 2 == 0:
        found[ring // 2] = jnp.concatenate([swap(above[:half], down), swap(below[half:], up)], axis=0)
    return found


def gather_plane(value, size):
    across = permutations(size)[3]
    near = gather_ring(value, size)
    return near + [swap(piece, across) for piece in near]


def gather_all(value, size):
    core = permutations(size)[4]
    near = jnp.concatenate([piece[None] for piece in gather_plane(value, size)], axis=0)
    return jnp.concatenate([near, swap(near, core)], axis=0)


def add(left, right):
    return left.astype(jnp.float32) + right.astype(jnp.float32)


def reduce_all(parts, size):
    ring, up, down, across, core = permutations(size)
    kind = parts.dtype
    count = size // 2
    mine = add(parts[:count], swap(parts[count:], core)).astype(kind)
    lines = [None] * ring
    order = sorted(range(ring), key=lambda r: -min(r, ring - r))
    for r in order:
        lines[r] = add(mine[r], swap(mine[ring + r], across))
    half = lines[0].shape[0] // 2
    if ring % 2 == 0:
        far = lines[ring // 2].astype(kind)
        low, high = swap(far[:half], up), swap(far[half:], down)
        last = ring // 2 - 1
        if last > 0:
            lines[last] = jnp.concatenate([add(lines[last][:half], low), lines[last][half:]], axis=0)
            other = ring - last
            lines[other] = jnp.concatenate([lines[other][:half], add(lines[other][half:], high)], axis=0)
        else:
            lines[0] = lines[0] + jnp.concatenate([low, high], axis=0).astype(jnp.float32)
    for step in range((ring - 1) // 2, 0, -1):
        low, high = swap(lines[step].astype(kind), up), swap(lines[ring - step].astype(kind), down)
        if step > 1:
            lines[step - 1], lines[ring - step + 1] = add(lines[step - 1], low), add(lines[ring - step + 1], high)
        else:
            lines[0] = lines[0] + low.astype(jnp.float32) + high.astype(jnp.float32)
    return lines[0]


def slot_devices(size, device):
    ring = size // 4
    slot = jnp.arange(size, dtype=jnp.int32)
    rc, ry, rz = slot // (2 * ring), (slot // ring) % 2, slot % ring
    z, y, c = device // 4, (device // 2) % 2, device % 2
    return ((z + rz) % ring) * 4 + (y ^ ry) * 2 + (c ^ rc)


def gathered_plan(
    hidden_in,
    queries,
    key_rows,
    value_rows,
    window_start,
    output_weight,
    norm_gain,
    expert_ids,
    route_weights,
    gate_weight,
    up_weight,
    down_weight,
):
    tok_count, width_d = hidden_in.shape
    head_dim = key_rows.shape[1] // KV_HEADS
    group_size = HEADS // KV_HEADS
    score_scale = head_dim ** (-0.5)
    size = lax.axis_size("seq")
    device = lax.axis_index("seq")
    part = lax.axis_index("grp")
    core_bit = device % 2
    ring, up, down, across, core = permutations(size)
    slots = slot_devices(size, device)

    half_d = width_d // 2
    own_columns = lax.dynamic_slice_in_dim(output_weight, part * half_d, half_d, 1)
    projection = gather_plane(own_columns, size)

    experts_all = size
    table = jnp.sum(
        jnp.where(
            expert_ids[:, :, None] == jnp.arange(experts_all, dtype=jnp.int32)[None, None, :],
            route_weights[:, :, None],
            0.0,
        ),
        axis=1,
    )
    table_high = table.astype(jnp.bfloat16)
    table_low = (table - table_high.astype(jnp.float32)).astype(jnp.bfloat16)
    kv_width = KV_HEADS * head_dim
    small = jnp.concatenate(
        [key_rows, value_rows, jnp.pad(jnp.concatenate([table_high, table_low], axis=1), ((0, 0), (0, 128 - 2 * experts_all)))],
        axis=1,
    )
    everything = gather_all(small, size)
    keys = everything[:, :, :kv_width].reshape(size * tok_count, KV_HEADS, head_dim)
    values = everything[:, :, kv_width : 2 * kv_width].reshape(size * tok_count, KV_HEADS, head_dim)
    tables = everything[:, :, 2 * kv_width :].astype(jnp.float32)
    picked = jnp.arange(128, dtype=jnp.int32)
    picked = (picked == device) | (picked == device + experts_all)
    scale = jnp.sum(jnp.where(picked[None, None, :], tables, 0.0), axis=-1, keepdims=True)

    query_pos = device * tok_count + jnp.arange(tok_count, dtype=jnp.int32)
    key_pos = (slots[:, None] * tok_count + jnp.arange(tok_count, dtype=jnp.int32)[None, :]).reshape(-1)
    allowed = (key_pos[None, :] <= query_pos[:, None]) & (key_pos[None, :] >= window_start[:, None])
    query_block = queries.reshape(tok_count, KV_HEADS, group_size, head_dim).transpose(1, 2, 0, 3)
    scores = (
        jnp.einsum("kgmd,nkd->kgmn", query_block, keys, preferred_element_type=jnp.float32) * score_scale
    )
    scores = jnp.where(allowed[None, None], scores, -1e30)
    row_max = jnp.max(scores, axis=-1, keepdims=True)
    expo = jnp.where(allowed[None, None], jnp.exp(scores - row_max), 0.0)
    denominator = jnp.sum(expo, axis=-1, keepdims=True)
    attended = jnp.einsum(
        "kgmn,nkd->kgmd", expo.astype(jnp.bfloat16), values, preferred_element_type=jnp.float32
    )
    attended = (attended / denominator).astype(jnp.bfloat16)

    attended = attended.reshape(HEADS // 2, 2, tok_count, head_dim)
    order = jnp.stack([slots[: size // 2] // 2]).reshape(-1)
    mine = jnp.take(attended[:, 0], order, axis=0), jnp.take(attended[:, 1], order, axis=0)
    kept = jnp.where(core_bit == 0, mine[0], mine[1])
    given = jnp.where(core_bit == 0, mine[1], mine[0])
    chip = jnp.concatenate([kept, swap(given, core)], axis=1)
    pair = lax.ppermute(chip, "grp", [(0, 1), (1, 0)])
    rows = jnp.concatenate([chip, pair], axis=1)
    weights = jnp.concatenate([piece[None] for piece in projection], axis=0)
    partial = jnp.einsum("htd,hdc->tc", rows, weights, preferred_element_type=jnp.float32)
    partial = partial.reshape(2, 2, tok_count, half_d)
    summed = partial[:, 0] + swap(partial[:, 1], core)
    own_half = summed[0]
    other_half = lax.ppermute(summed[1].astype(jnp.bfloat16), "grp", [(0, 1), (1, 0)]).astype(jnp.float32)
    projected = jnp.where(
        part == 0,
        jnp.concatenate([own_half, other_half], axis=1),
        jnp.concatenate([other_half, own_half], axis=1),
    )
    residual = (hidden_in.astype(jnp.float32) + projected).astype(jnp.bfloat16)
    resid_float = residual.astype(jnp.float32)
    normed = (
        resid_float
        * lax.rsqrt(jnp.mean(resid_float * resid_float, axis=-1, keepdims=True) + 1e-06)
        * norm_gain
    ).astype(jnp.bfloat16)

    results = []
    chunk = tok_count // CHUNKS
    for start in range(0, tok_count, chunk):
        tokens = gather_all(normed[start : start + chunk], size)
        inputs = tokens.reshape(size * chunk, width_d)
        gate_out = jnp.dot(inputs, gate_weight[0], preferred_element_type=jnp.float32)
        up_out = jnp.dot(inputs, up_weight[0], preferred_element_type=jnp.float32)
        inner = (jax.nn.silu(gate_out) * up_out).astype(jnp.bfloat16)
        out = jnp.dot(inner, down_weight[0], preferred_element_type=jnp.float32)
        out = out.reshape(size, chunk, width_d) * scale[:, start : start + chunk]
        results.append(reduce_all(out.astype(jnp.bfloat16), size))
    mixture = jnp.concatenate(results, axis=0) if len(results) > 1 else results[0]
    return (resid_float + mixture).astype(jnp.bfloat16)


def on_device(*arrays):
    experts_all = lax.axis_size("seq") * arrays[9].shape[0]
    dense = experts_all <= 2 * arrays[7].shape[1]
    paired = lax.axis_size("grp") == 2 and lax.axis_size("seq") % 4 == 0
    one_head = arrays[5].shape[0] == arrays[2].shape[1] // KV_HEADS and arrays[9].shape[0] == 1
    if dense and paired and one_head:
        return gathered_plan(*arrays)
    return spread_out(*arrays)


def solution(mesh):
    return jax.shard_map(
        on_device,
        mesh=mesh,
        in_specs=(
            P(("grp", "seq"), None),
            P(("grp", "seq"), None),
            P(("grp", "seq"), None),
            P(("grp", "seq"), None),
            P(("grp", "seq")),
            P("seq", None),
            P(),
            P(("grp", "seq"), None),
            P(("grp", "seq"), None),
            P("seq", None, None),
            P("seq", None, None),
            P("seq", None, None),
        ),
        out_specs=P(("grp", "seq"), None),
        check_vma=False,
    )
```

```python
import jax
import jax.numpy as jnp
from jax import lax
from jax.experimental import pallas as pl
from jax.experimental.pallas import tpu as pltpu
from jax.sharding import PartitionSpec as P

HEADS = 16
KV_HEADS = 2


def spread_out(
    hidden_in,
    queries,
    key_rows,
    value_rows,
    window_start,
    output_weight,
    norm_gain,
    expert_ids,
    route_weights,
    gate_weight,
    up_weight,
    down_weight,
):
    tok_count = queries.shape[0]
    width_d = hidden_in.shape[1]
    head_dim = key_rows.shape[1] // KV_HEADS
    group_size = HEADS // KV_HEADS
    score_scale = head_dim ** (-0.5)
    device = lax.axis_index("seq")
    first_pos = device * tok_count
    query_pos = first_pos + jnp.arange(tok_count, dtype=jnp.int32)
    last_pos = first_pos + tok_count - 1
    first_start = window_start[0]
    query_block = (
        queries.reshape(tok_count, KV_HEADS, group_size, head_dim)
        .transpose(1, 2, 0, 3)
        .reshape(KV_HEADS, group_size * tok_count, head_dim)
    )
    query_rows = group_size * tok_count

    def attend(running, key_block, value_block, block_start):
        row_max, denominator, accumulated = running
        scores = (
            jnp.einsum("kmd,nkd->kmn", query_block, key_block, preferred_element_type=jnp.float32)
            * score_scale
        )
        key_pos = block_start + jnp.arange(key_block.shape[0], dtype=jnp.int32)
        allowed = (key_pos[None, :] <= query_pos[:, None]) & (
            key_pos[None, :] >= window_start[:, None]
        )
        allowed = jnp.tile(allowed, (group_size, 1))[None]
        scores = jnp.where(allowed, scores, -1e30)
        newest = jnp.maximum(row_max, jnp.max(scores, axis=-1))
        factor = jnp.exp(row_max - newest)
        weights = jnp.where(allowed, jnp.exp(scores - newest[..., None]), 0.0)
        denominator = denominator * factor + jnp.sum(weights, axis=-1)
        accumulated = accumulated * factor[..., None] + jnp.einsum(
            "kmn,nkd->kmd",
            weights.astype(jnp.bfloat16),
            value_block,
            preferred_element_type=jnp.float32,
        )
        return (newest, denominator, accumulated)

    initial = (
        jnp.full((KV_HEADS, query_rows), -1e30, jnp.float32),
        jnp.zeros((KV_HEADS, query_rows), jnp.float32),
        jnp.zeros((KV_HEADS, query_rows, head_dim), jnp.float32),
    )
    running = initial
    key_piece = lax.all_gather(key_rows, "seq", axis=0, tiled=True)
    value_piece = lax.all_gather(value_rows, "seq", axis=0, tiled=True)
    row_count = key_piece.shape[0]
    block_size = 512
    block_count = row_count // block_size
    key_blocks = key_piece.reshape(block_count, block_size, KV_HEADS, head_dim)
    value_blocks = value_piece.reshape(block_count, block_size, KV_HEADS, head_dim)

    def one_block(carried, block_index):
        block_start = block_index * block_size
        needed = (block_start <= last_pos) & (block_start + block_size - 1 >= first_start)
        carried = lax.cond(
            needed,
            lambda inner_state: attend(
                inner_state, key_blocks[block_index], value_blocks[block_index], block_start
            ),
            lambda inner_state: inner_state,
            carried,
        )
        return (carried, None)

    running, unused = lax.scan(one_block, running, jnp.arange(block_count, dtype=jnp.int32))
    row_max, denominator, accumulated = running
    attended = (
        (accumulated / denominator[..., None])
        .reshape(KV_HEADS, group_size, tok_count, head_dim)
        .transpose(2, 0, 1, 3)
        .reshape(tok_count, HEADS * head_dim)
        .astype(jnp.bfloat16)
    )
    projected = jnp.dot(
        attended,
        lax.all_gather(output_weight, "seq", axis=0, tiled=True),
        preferred_element_type=jnp.float32,
    )
    residual = (hidden_in.astype(jnp.float32) + projected).astype(jnp.bfloat16)
    resid_float = residual.astype(jnp.float32)
    normed = (
        resid_float
        * lax.rsqrt(jnp.mean(resid_float * resid_float, axis=-1, keepdims=True) + 1e-06)
        * norm_gain
    ).astype(jnp.bfloat16)
    top_count = expert_ids.shape[1]
    local_experts = gate_weight.shape[0]
    devices = lax.axis_size("seq")
    experts_all = devices * local_experts
    capacity = max(2, 3 * tok_count * top_count // (2 * experts_all))
    flat_ids = expert_ids.reshape(-1)
    onehot = (flat_ids[:, None] == jnp.arange(experts_all, dtype=jnp.int32)[None, :]).astype(
        jnp.int32
    )
    slot_rank = jnp.sum((jnp.cumsum(onehot, axis=0) - 1) * onehot, axis=1)
    destination = flat_ids * capacity + slot_rank
    slot_rows = jnp.repeat(normed, top_count, axis=0)
    outgoing = (
        jnp.zeros((experts_all * capacity, width_d), jnp.bfloat16).at[destination].set(slot_rows)
    )
    outgoing = outgoing.reshape(devices, local_experts, capacity, width_d)
    arrived = lax.all_to_all(outgoing, "seq", split_axis=0, concat_axis=0, tiled=True)
    inputs = arrived[:, 0].reshape(-1, width_d)
    gate_out = jnp.dot(inputs, gate_weight[0], preferred_element_type=jnp.float32)
    up_out = jnp.dot(inputs, up_weight[0], preferred_element_type=jnp.float32)
    inner = (jax.nn.silu(gate_out) * up_out).astype(jnp.bfloat16)
    result = jnp.dot(inner, down_weight[0], preferred_element_type=jnp.float32).astype(jnp.bfloat16)
    outputs = [result.reshape(arrived.shape[0], arrived.shape[2], width_d)]
    computed = jnp.stack(outputs, axis=1)
    returned = lax.all_to_all(computed, "seq", split_axis=0, concat_axis=0, tiled=True)
    gathered = (
        returned.reshape(experts_all * capacity, width_d)[destination]
        .astype(jnp.float32)
        .reshape(tok_count, top_count, width_d)
    )
    mixture = jnp.sum(gathered * route_weights[..., None], axis=1)
    return (resid_float + mixture).astype(jnp.bfloat16)


def swap(value, perm):
    return lax.ppermute(value, "seq", perm)


def after(value, *others):
    return lax.optimization_barrier((value, *others))[0]


def exchanges(size):
    forth = [(i, (i + 4) % size if i % 2 == 0 else (i - 4) % size) for i in range(size)]
    back = [(j, i) for i, j in forth]
    across = [(i, i ^ 2) for i in range(size)]
    core = [(i, i ^ 1) for i in range(size)]
    return forth, back, across, core


def gather_near(value, size, early=None, late=None):
    forth, back, across, core = exchanges(size)
    first = value if early is None else after(value, early)
    same = swap(first, forth)
    peer = swap(first, core)
    other = swap(peer, forth)
    far = swap(same, forth)
    own = value if late is None else after(value, late)
    line = [own, same, other, far]
    return line, [swap(piece, across) for piece in line], same, far


def stack(pieces):
    return jnp.concatenate([piece[None] for piece in pieces], axis=0)


def add(left, right):
    return left.astype(jnp.float32) + right.astype(jnp.float32)


def reduce_all(near, far, size):
    forth, back, across, core = exchanges(size)
    kind = near.dtype
    mine = add(near, swap(far, core))
    line = [None] * 4
    for j in (3, 2, 1, 0):
        line[j] = mine[j] + swap(mine[4 + j].astype(kind), across).astype(jnp.float32)
    same = line[1] + swap(line[3].astype(kind), back).astype(jnp.float32)
    other = swap(swap(line[2].astype(kind), back), core)
    return line[0] + other.astype(jnp.float32) + swap(same.astype(kind), back).astype(jnp.float32)


def slot_device(size, device, slot):
    ring = size // 4
    z, y, c = device // 4, (device // 2) % 2, device % 2
    c = c ^ (slot // 8)
    step = 2 * c - 1
    dz, dc = ((0, 0), (step, 0), (step, 1), (2 * step, 0))[slot % 4]
    return ((z + dz + ring) % ring) * 4 + (y ^ (slot // 4 % 2)) * 2 + (c ^ dc)


def attention(queries, near, far, window_start, device, size, kv_width):
    tok_count, width = queries.shape
    head_dim = width // HEADS
    group_size = HEADS // KV_HEADS
    score_scale = head_dim ** (-0.5)
    count = size * tok_count
    half = count // 2
    pair = 2 * tok_count

    def body(device_ref, queries_ref, near_ref, far_ref, start_ref, kept_ref, given_ref, mask_ref, out_ref):
        device = device_ref[0]
        lane = lax.broadcasted_iota(jnp.int32, (tok_count, pair), 1)
        query_pos = device * tok_count + lax.broadcasted_iota(jnp.int32, (tok_count, pair), 0)
        start = start_ref[...]
        for block in range(size // 2):
            first = slot_device(size, device, 2 * block) * tok_count
            second = slot_device(size, device, 2 * block + 1) * tok_count - tok_count
            key_pos = jnp.where(lane < tok_count, first, second) + lane
            seen = (key_pos <= query_pos) & (key_pos >= start)
            mask_ref[:, block * pair : (block + 1) * pair] = seen.astype(jnp.int32)
        for two in range(HEADS // 2):
            group = 2 * two // group_size
            mask = mask_ref[...] != 0
            mask = jnp.concatenate([mask_ref[...], mask_ref[...]], axis=0) != 0
            rows = jnp.concatenate(
                [
                    queries_ref[:, 2 * two * head_dim : (2 * two + 1) * head_dim],
                    queries_ref[:, (2 * two + 1) * head_dim : (2 * two + 2) * head_dim],
                ],
                axis=0,
            )
            key_at = slice(group * head_dim, (group + 1) * head_dim)
            value_at = slice(kv_width + group * head_dim, kv_width + (group + 1) * head_dim)
            contract = (((1,), (1,)), ((), ()))
            scores = jnp.concatenate(
                [
                    lax.dot_general(rows, ref[:, :, key_at].reshape(half, head_dim), contract, preferred_element_type=jnp.float32)
                    for ref in (near_ref, far_ref)
                ],
                axis=1,
            )
            scores = jnp.where(mask, scores * score_scale, -1e30)
            row_max = jnp.max(scores, axis=-1, keepdims=True)
            expo = jnp.where(mask, jnp.exp(scores - row_max), 0.0)
            denominator = jnp.sum(expo, axis=-1, keepdims=True)
            probs = expo.astype(jnp.bfloat16)
            summed = jnp.dot(
                probs[:, :half], near_ref[:, :, value_at].reshape(half, head_dim), preferred_element_type=jnp.float32
            ) + jnp.dot(probs[:, half:], far_ref[:, :, value_at].reshape(half, head_dim), preferred_element_type=jnp.float32)
            result = (summed / denominator).astype(jnp.bfloat16)
            out_ref[2 * two] = result[:tok_count]
            out_ref[2 * two + 1] = result[tok_count:]
        for slot in range(size // 2):
            kept_ref[slot] = out_ref[slot_device(size, device, slot)]
            given_ref[slot] = out_ref[slot_device(size, device, slot + size // 2)]

    shape = jax.ShapeDtypeStruct((size // 2, tok_count, head_dim), jnp.bfloat16)
    vmem = pl.BlockSpec(memory_space=pltpu.VMEM)
    return pl.pallas_call(
        body,
        out_shape=(shape, shape),
        in_specs=[pl.BlockSpec(memory_space=pltpu.SMEM), vmem, vmem, vmem, vmem],
        out_specs=(vmem, vmem),
        scratch_shapes=[
            pltpu.VMEM((tok_count, count), jnp.int32),
            pltpu.VMEM((HEADS, tok_count, head_dim), jnp.bfloat16),
        ],
        name="attention",
    )(device[None], queries, near, far, window_start[:, None])


def project(kept, got, kept_pair, got_pair, weights):
    slots, tok_count, head_dim = kept.shape
    columns = weights[0].shape[1]

    def body(kept_ref, got_ref, kept_pair_ref, got_pair_ref, *refs):
        weight_refs, (own_ref, pair_ref, given_ref) = refs[:slots], refs[slots:]
        total = None
        for slot in range(slots):
            rows = jnp.concatenate(
                [kept_ref[slot], kept_pair_ref[slot], got_ref[slot], got_pair_ref[slot]], axis=0
            )
            term = jnp.dot(rows, weight_refs[slot][...], preferred_element_type=jnp.float32)
            total = term if total is None else total + term
        own_ref[...] = total[:tok_count]
        pair_ref[...] = total[tok_count : 2 * tok_count]
        given_ref[...] = total[2 * tok_count :]

    vmem = pl.BlockSpec(memory_space=pltpu.VMEM)
    one = jax.ShapeDtypeStruct((tok_count, columns), jnp.float32)
    return pl.pallas_call(
        body,
        out_shape=(one, one, jax.ShapeDtypeStruct((2 * tok_count, columns), jnp.float32)),
        in_specs=[vmem] * (4 + slots),
        out_specs=(vmem, vmem, vmem),
        name="project",
    )(kept, got, kept_pair, got_pair, *weights)


def gathered_plan(
    hidden_in,
    queries,
    key_rows,
    value_rows,
    window_start,
    output_weight,
    norm_gain,
    expert_ids,
    route_weights,
    gate_weight,
    up_weight,
    down_weight,
):
    tok_count, width_d = hidden_in.shape
    head_dim = key_rows.shape[1] // KV_HEADS
    size = lax.axis_size("seq")
    device = lax.axis_index("seq")
    part = lax.axis_index("grp")
    forth, back, across, core = exchanges(size)

    experts_all = size
    table = jnp.sum(
        jnp.where(
            expert_ids[:, :, None] == jnp.arange(experts_all, dtype=jnp.int32)[None, None, :],
            route_weights[:, :, None],
            0.0,
        ),
        axis=1,
    )
    table_high = table.astype(jnp.bfloat16)
    table_low = (table - table_high.astype(jnp.float32)).astype(jnp.bfloat16)
    kv_width = KV_HEADS * head_dim
    small = jnp.concatenate(
        [key_rows, value_rows, jnp.pad(jnp.concatenate([table_high, table_low], axis=1), ((0, 0), (0, 128 - 2 * experts_all)))],
        axis=1,
    )
    line, side, same_small, far_small = gather_near(small, size)
    near_small = stack(line + side)
    far_near = swap(near_small, core)

    half_d = width_d // 2
    own_columns = lax.dynamic_slice_in_dim(output_weight, part * half_d, half_d, 1)
    line, side, _, _ = gather_near(own_columns, size, same_small, far_small)
    projection = line + side

    other_part = [(0, 1), (1, 0)]
    kept, given = attention(after(queries, far_small), near_small, far_near, window_start, device, size, kv_width)
    got = swap(given, core)
    kept_pair = lax.ppermute(kept, "grp", other_part)
    got_pair = lax.ppermute(got, "grp", other_part)
    own, pair, sent = project(kept, got, kept_pair, got_pair, projection)
    back_sum = swap(sent, core)
    own_half = own + back_sum[:tok_count]
    pair_half = (pair + back_sum[tok_count:]).astype(jnp.bfloat16)
    other_half = lax.ppermute(pair_half, "grp", other_part).astype(jnp.float32)
    projected = jnp.where(
        part == 0,
        jnp.concatenate([own_half, other_half], axis=1),
        jnp.concatenate([other_half, own_half], axis=1),
    )
    residual = (hidden_in.astype(jnp.float32) + projected).astype(jnp.bfloat16)
    resid_float = residual.astype(jnp.float32)
    normed = (
        resid_float
        * lax.rsqrt(jnp.mean(resid_float * resid_float, axis=-1, keepdims=True) + 1e-06)
        * norm_gain
    ).astype(jnp.bfloat16)

    picked = jnp.arange(128, dtype=jnp.int32)
    picked = (picked == device) | (picked == device + experts_all)

    def routed(small):
        tables = small[:, :, 2 * kv_width :].astype(jnp.float32)
        return jnp.sum(jnp.where(picked[None, None, :], tables, 0.0), axis=-1, keepdims=True)

    def expert(tokens, weights):
        inputs = tokens.reshape(-1, width_d)
        gate_out = jnp.dot(inputs, gate_weight[0], preferred_element_type=jnp.float32)
        up_out = jnp.dot(inputs, up_weight[0], preferred_element_type=jnp.float32)
        inner = (jax.nn.silu(gate_out) * up_out).astype(jnp.bfloat16)
        out = jnp.dot(inner, down_weight[0], preferred_element_type=jnp.float32)
        return (out.reshape(tokens.shape) * weights).astype(jnp.bfloat16)

    line, side, _, _ = gather_near(normed, size)
    near = stack(line + side)
    far = swap(near, core)
    near_out = expert(near, routed(near_small))
    far_out = expert(far, routed(far_near))
    mixture = reduce_all(near_out, far_out, size)
    return (resid_float + mixture).astype(jnp.bfloat16)


def on_device(*arrays):
    size = lax.axis_size("seq")
    dense = size * arrays[9].shape[0] <= 2 * arrays[7].shape[1]
    placed = lax.axis_size("grp") == 2 and size == 16 and arrays[9].shape[0] == 1
    one_head = arrays[5].shape[0] * KV_HEADS == arrays[2].shape[1]
    if dense and placed and one_head:
        return gathered_plan(*arrays)
    return spread_out(*arrays)


def solution(mesh):
    return jax.shard_map(
        on_device,
        mesh=mesh,
        in_specs=(
            P(("grp", "seq"), None),
            P(("grp", "seq"), None),
            P(("grp", "seq"), None),
            P(("grp", "seq"), None),
            P(("grp", "seq")),
            P("seq", None),
            P(),
            P(("grp", "seq"), None),
            P(("grp", "seq"), None),
            P("seq", None, None),
            P("seq", None, None),
            P("seq", None, None),
        ),
        out_specs=P(("grp", "seq"), None),
        check_vma=False,
    )
```

```python
import jax
import jax.numpy as jnp
from jax import lax
from jax.experimental import pallas as pl
from jax.experimental.pallas import tpu as pltpu
from jax.sharding import PartitionSpec as P

HEADS = 16
KV_HEADS = 2


def spread_out(
    hidden_in,
    queries,
    key_rows,
    value_rows,
    window_start,
    output_weight,
    norm_gain,
    expert_ids,
    route_weights,
    gate_weight,
    up_weight,
    down_weight,
):
    tok_count = queries.shape[0]
    width_d = hidden_in.shape[1]
    head_dim = key_rows.shape[1] // KV_HEADS
    group_size = HEADS // KV_HEADS
    score_scale = head_dim ** (-0.5)
    device = lax.axis_index("seq")
    first_pos = device * tok_count
    query_pos = first_pos + jnp.arange(tok_count, dtype=jnp.int32)
    last_pos = first_pos + tok_count - 1
    first_start = window_start[0]
    query_block = (
        queries.reshape(tok_count, KV_HEADS, group_size, head_dim)
        .transpose(1, 2, 0, 3)
        .reshape(KV_HEADS, group_size * tok_count, head_dim)
    )
    query_rows = group_size * tok_count

    def attend(running, key_block, value_block, block_start):
        row_max, denominator, accumulated = running
        scores = (
            jnp.einsum("kmd,nkd->kmn", query_block, key_block, preferred_element_type=jnp.float32)
            * score_scale
        )
        key_pos = block_start + jnp.arange(key_block.shape[0], dtype=jnp.int32)
        allowed = (key_pos[None, :] <= query_pos[:, None]) & (
            key_pos[None, :] >= window_start[:, None]
        )
        allowed = jnp.tile(allowed, (group_size, 1))[None]
        scores = jnp.where(allowed, scores, -1e30)
        newest = jnp.maximum(row_max, jnp.max(scores, axis=-1))
        factor = jnp.exp(row_max - newest)
        weights = jnp.where(allowed, jnp.exp(scores - newest[..., None]), 0.0)
        denominator = denominator * factor + jnp.sum(weights, axis=-1)
        accumulated = accumulated * factor[..., None] + jnp.einsum(
            "kmn,nkd->kmd",
            weights.astype(jnp.bfloat16),
            value_block,
            preferred_element_type=jnp.float32,
        )
        return (newest, denominator, accumulated)

    initial = (
        jnp.full((KV_HEADS, query_rows), -1e30, jnp.float32),
        jnp.zeros((KV_HEADS, query_rows), jnp.float32),
        jnp.zeros((KV_HEADS, query_rows, head_dim), jnp.float32),
    )
    running = initial
    key_piece = lax.all_gather(key_rows, "seq", axis=0, tiled=True)
    value_piece = lax.all_gather(value_rows, "seq", axis=0, tiled=True)
    row_count = key_piece.shape[0]
    block_size = 512
    block_count = row_count // block_size
    key_blocks = key_piece.reshape(block_count, block_size, KV_HEADS, head_dim)
    value_blocks = value_piece.reshape(block_count, block_size, KV_HEADS, head_dim)

    def one_block(carried, block_index):
        block_start = block_index * block_size
        needed = (block_start <= last_pos) & (block_start + block_size - 1 >= first_start)
        carried = lax.cond(
            needed,
            lambda inner_state: attend(
                inner_state, key_blocks[block_index], value_blocks[block_index], block_start
            ),
            lambda inner_state: inner_state,
            carried,
        )
        return (carried, None)

    running, _ = lax.scan(one_block, running, jnp.arange(block_count, dtype=jnp.int32))
    _, denominator, accumulated = running
    attended = (
        (accumulated / denominator[..., None])
        .reshape(KV_HEADS, group_size, tok_count, head_dim)
        .transpose(2, 0, 1, 3)
        .reshape(tok_count, HEADS * head_dim)
        .astype(jnp.bfloat16)
    )
    projected = jnp.dot(
        attended,
        lax.all_gather(output_weight, "seq", axis=0, tiled=True),
        preferred_element_type=jnp.float32,
    )
    residual = (hidden_in.astype(jnp.float32) + projected).astype(jnp.bfloat16)
    resid_float = residual.astype(jnp.float32)
    normed = (
        resid_float
        * lax.rsqrt(jnp.mean(resid_float * resid_float, axis=-1, keepdims=True) + 1e-06)
        * norm_gain
    ).astype(jnp.bfloat16)
    top_count = expert_ids.shape[1]
    local_experts = gate_weight.shape[0]
    devices = lax.axis_size("seq")
    experts_all = devices * local_experts
    capacity = max(2, 3 * tok_count * top_count // (2 * experts_all))
    flat_ids = expert_ids.reshape(-1)
    onehot = (flat_ids[:, None] == jnp.arange(experts_all, dtype=jnp.int32)[None, :]).astype(
        jnp.int32
    )
    slot_rank = jnp.sum((jnp.cumsum(onehot, axis=0) - 1) * onehot, axis=1)
    destination = flat_ids * capacity + slot_rank
    slot_rows = jnp.repeat(normed, top_count, axis=0)
    outgoing = (
        jnp.zeros((experts_all * capacity, width_d), jnp.bfloat16).at[destination].set(slot_rows)
    )
    outgoing = outgoing.reshape(devices, local_experts, capacity, width_d)
    arrived = lax.all_to_all(outgoing, "seq", split_axis=0, concat_axis=0, tiled=True)
    inputs = arrived[:, 0].reshape(-1, width_d)
    gate_out = jnp.dot(inputs, gate_weight[0], preferred_element_type=jnp.float32)
    up_out = jnp.dot(inputs, up_weight[0], preferred_element_type=jnp.float32)
    inner = (jax.nn.silu(gate_out) * up_out).astype(jnp.bfloat16)
    result = jnp.dot(inner, down_weight[0], preferred_element_type=jnp.float32).astype(jnp.bfloat16)
    outputs = [result.reshape(arrived.shape[0], arrived.shape[2], width_d)]
    computed = jnp.stack(outputs, axis=1)
    returned = lax.all_to_all(computed, "seq", split_axis=0, concat_axis=0, tiled=True)
    gathered = (
        returned.reshape(experts_all * capacity, width_d)[destination]
        .astype(jnp.float32)
        .reshape(tok_count, top_count, width_d)
    )
    mixture = jnp.sum(gathered * route_weights[..., None], axis=1)
    return (resid_float + mixture).astype(jnp.bfloat16)


def swap(value, perm, axis="seq"):
    return lax.ppermute(value, axis, perm)


def after(value, *others):
    return lax.optimization_barrier((value, *others))[0]


def exchanges(size):
    forth = [(i, (i + 4) % size if i % 2 == 0 else (i - 4) % size) for i in range(size)]
    back = [(j, i) for i, j in forth]
    across = [(i, i ^ 2) for i in range(size)]
    core = [(i, i ^ 1) for i in range(size)]
    opposite = [(i, (i + size // 2) % size) for i in range(size)]
    return forth, back, across, core, opposite


def slot_device(size, device, slot):
    ring = size // 4
    z, y, c = device // 4, (device // 2) % 2, device % 2
    c = c ^ (slot // 8)
    step = 2 * c - 1
    dz, dc = ((0, 0), (step, 0), (step, 1), (2 * step, 0))[slot % 4]
    return ((z + dz + ring) % ring) * 4 + (y ^ (slot // 4 % 2)) * 2 + (c ^ dc)


def attention(queries, pieces, window_start, device, size, kv_width):
    tok_count, width = queries.shape
    head_dim = width // HEADS
    group_size = HEADS // KV_HEADS
    score_scale = head_dim ** (-0.5)
    count = size * tok_count
    pair = 2 * tok_count

    def body(device_ref, queries_ref, start_ref, *refs):
        piece_refs, (kept_ref, given_ref, mask_ref, out_ref) = refs[:size], refs[size:]
        device = device_ref[0]
        lane = lax.broadcasted_iota(jnp.int32, (tok_count, pair), 1)
        query_pos = device * tok_count + lax.broadcasted_iota(jnp.int32, (tok_count, pair), 0)
        start = start_ref[...]
        for block in range(size // 2):
            first = slot_device(size, device, 2 * block) * tok_count
            second = slot_device(size, device, 2 * block + 1) * tok_count - tok_count
            key_pos = jnp.where(lane < tok_count, first, second) + lane
            seen = (key_pos <= query_pos) & (key_pos >= start)
            mask_ref[:, block * pair : (block + 1) * pair] = seen.astype(jnp.int32)
        for group in range(KV_HEADS):
            key_at = slice(group * head_dim, (group + 1) * head_dim)
            value_at = slice(kv_width + group * head_dim, kv_width + (group + 1) * head_dim)
            keys = jnp.concatenate([ref[:, key_at] for ref in piece_refs], axis=0)
            values = jnp.concatenate([ref[:, value_at] for ref in piece_refs], axis=0)
            for two in range(group * group_size // 2, (group + 1) * group_size // 2):
                mask = jnp.concatenate([mask_ref[...], mask_ref[...]], axis=0) != 0
                rows = jnp.concatenate(
                    [queries_ref[:, h * head_dim : (h + 1) * head_dim] for h in (2 * two, 2 * two + 1)], axis=0
                )
                scores = lax.dot_general(
                    rows, keys, (((1,), (1,)), ((), ())), preferred_element_type=jnp.float32
                )
                scores = jnp.where(mask, scores * score_scale, -1e30)
                row_max = jnp.max(scores, axis=-1, keepdims=True)
                expo = jnp.where(mask, jnp.exp(scores - row_max), 0.0)
                denominator = jnp.sum(expo, axis=-1, keepdims=True)
                summed = jnp.dot(expo.astype(jnp.bfloat16), values, preferred_element_type=jnp.float32)
                result = (summed / denominator).astype(jnp.bfloat16)
                out_ref[2 * two] = result[:tok_count]
                out_ref[2 * two + 1] = result[tok_count:]
        for slot in range(size // 2):
            kept_ref[slot] = out_ref[slot_device(size, device, slot)]
            given_ref[slot] = out_ref[slot_device(size, device, slot + size // 2)]

    shape = jax.ShapeDtypeStruct((size // 2, tok_count, head_dim), jnp.bfloat16)
    vmem = pl.BlockSpec(memory_space=pltpu.VMEM)
    return pl.pallas_call(
        body,
        out_shape=(shape, shape),
        in_specs=[pl.BlockSpec(memory_space=pltpu.SMEM)] + [vmem] * (2 + size),
        out_specs=(vmem, vmem),
        scratch_shapes=[
            pltpu.VMEM((tok_count, count), jnp.int32),
            pltpu.VMEM((HEADS, tok_count, head_dim), jnp.bfloat16),
        ],
        compiler_params=pltpu.CompilerParams(vmem_limit_bytes=12 << 20),
        name="attention",
    )(device[None], queries, window_start[:, None], *pieces)


def project(kept, got, kept_pair, got_pair, weights):
    slots, tok_count, _ = kept.shape
    columns = weights[0].shape[1]

    def body(kept_ref, got_ref, kept_pair_ref, got_pair_ref, *refs):
        weight_refs, (own_ref, pair_ref, given_ref) = refs[:slots], refs[slots:]
        total = None
        for slot in range(slots):
            rows = jnp.concatenate(
                [kept_ref[slot], kept_pair_ref[slot], got_ref[slot], got_pair_ref[slot]], axis=0
            )
            term = jnp.dot(rows, weight_refs[slot][...], preferred_element_type=jnp.float32)
            total = term if total is None else total + term
        own_ref[...] = total[:tok_count]
        pair_ref[...] = total[tok_count : 2 * tok_count]
        given_ref[...] = total[2 * tok_count :]

    vmem = pl.BlockSpec(memory_space=pltpu.VMEM)
    one = jax.ShapeDtypeStruct((tok_count, columns), jnp.float32)
    return pl.pallas_call(
        body,
        out_shape=(one, one, jax.ShapeDtypeStruct((2 * tok_count, columns), jnp.float32)),
        in_specs=[vmem] * (4 + slots),
        out_specs=(vmem, vmem, vmem),
        compiler_params=pltpu.CompilerParams(vmem_limit_bytes=10 << 20),
        name="project",
    )(kept, got, kept_pair, got_pair, *weights)


def halves(own, pair, back):
    tok_count, _ = own.shape

    def body(own_ref, pair_ref, back_ref, kept_ref, sent_ref):
        kept_ref[...] = own_ref[...] + back_ref[:tok_count]
        sent_ref[...] = (pair_ref[...] + back_ref[tok_count:]).astype(jnp.bfloat16)

    vmem = pl.BlockSpec(memory_space=pltpu.VMEM)
    return pl.pallas_call(
        body,
        out_shape=(
            jax.ShapeDtypeStruct(own.shape, jnp.float32),
            jax.ShapeDtypeStruct(own.shape, jnp.bfloat16),
        ),
        in_specs=[vmem] * 3,
        out_specs=(vmem, vmem),
        compiler_params=pltpu.CompilerParams(vmem_limit_bytes=3 << 20),
        name="halves",
    )(own, pair, back)


def normalise(hidden_in, own_half, other_half, norm_gain, part):
    _, width_d = hidden_in.shape
    half_d = width_d // 2

    def body(part_ref, hidden_ref, own_ref, other_ref, gain_ref, resid_ref, normed_ref):
        own, other = own_ref[...], other_ref[...].astype(jnp.float32)
        first = part_ref[0] == 0
        low, high = jnp.where(first, own, other), jnp.where(first, other, own)
        low = (hidden_ref[:, :half_d].astype(jnp.float32) + low).astype(jnp.bfloat16)
        high = (hidden_ref[:, half_d:].astype(jnp.float32) + high).astype(jnp.bfloat16)
        resid_ref[:, :half_d] = low
        resid_ref[:, half_d:] = high
        low, high = low.astype(jnp.float32), high.astype(jnp.float32)
        square = jnp.sum(low * low, axis=-1, keepdims=True) + jnp.sum(high * high, axis=-1, keepdims=True)
        factor = lax.rsqrt(square / width_d + 1e-06)
        normed_ref[:, :half_d] = (low * factor * gain_ref[:, :half_d]).astype(jnp.bfloat16)
        normed_ref[:, half_d:] = (high * factor * gain_ref[:, half_d:]).astype(jnp.bfloat16)

    vmem = pl.BlockSpec(memory_space=pltpu.VMEM)
    shape = jax.ShapeDtypeStruct(hidden_in.shape, jnp.bfloat16)
    return pl.pallas_call(
        body,
        out_shape=(shape, shape),
        in_specs=[pl.BlockSpec(memory_space=pltpu.SMEM)] + [vmem] * 4,
        out_specs=(vmem, vmem),
        compiler_params=pltpu.CompilerParams(vmem_limit_bytes=3 << 20),
        name="normalise",
    )(part[None], hidden_in, own_half, other_half, norm_gain[None])


def expert(pieces, small, gate, up, down, device, table_at):
    tok_count, width_d = pieces[0].shape
    experts_all = lax.axis_size("seq")
    count = len(pieces)
    tile = 4 if count % 4 == 0 else count

    def body(device_ref, gate_ref, up_ref, down_ref, *refs):
        token_refs, small_refs, out_refs = refs[:count], refs[count : 2 * count], refs[2 * count :]
        lane = lax.broadcasted_iota(jnp.int32, (tok_count, 128), 1)
        picked = (lane == device_ref[0]) | (lane == device_ref[0] + experts_all)
        for first in range(0, count, tile):
            rows = jnp.concatenate([ref[...] for ref in token_refs[first : first + tile]], axis=0)
            gate_out = jnp.dot(rows, gate_ref[...], preferred_element_type=jnp.float32)
            up_out = jnp.dot(rows, up_ref[...], preferred_element_type=jnp.float32)
            inner = (gate_out / (1.0 + jnp.exp(-gate_out)) * up_out).astype(jnp.bfloat16)
            out = jnp.dot(inner, down_ref[...], preferred_element_type=jnp.float32)
            for at in range(tile):
                table = small_refs[first + at][:, table_at : table_at + 128].astype(jnp.float32)
                weight = jnp.sum(jnp.where(picked, table, 0.0), axis=-1, keepdims=True)
                out_refs[first + at][...] = (out[at * tok_count : (at + 1) * tok_count] * weight).astype(jnp.bfloat16)

    vmem = pl.BlockSpec(memory_space=pltpu.VMEM)
    shape = jax.ShapeDtypeStruct((tok_count, width_d), jnp.bfloat16)
    return pl.pallas_call(
        body,
        out_shape=[shape] * count,
        in_specs=[pl.BlockSpec(memory_space=pltpu.SMEM)] + [vmem] * (3 + 2 * count),
        out_specs=[vmem] * count,
        compiler_params=pltpu.CompilerParams(vmem_limit_bytes=26 << 20),
        name="expert",
    )(device[None], gate, up, down, *pieces, *small)


def add(left, right):
    return left.astype(jnp.float32) + right.astype(jnp.float32)


def gathered_plan(
    hidden_in,
    queries,
    key_rows,
    value_rows,
    window_start,
    output_weight,
    norm_gain,
    expert_ids,
    route_weights,
    gate_weight,
    up_weight,
    down_weight,
):
    _, width_d = hidden_in.shape
    head_dim = key_rows.shape[1] // KV_HEADS
    size = lax.axis_size("seq")
    device = lax.axis_index("seq")
    part = lax.axis_index("grp")
    forth, back, across, core, opposite = exchanges(size)
    other_part = [(0, 1), (1, 0)]

    experts_all = size
    table = jnp.sum(
        jnp.where(
            expert_ids[:, :, None] == jnp.arange(experts_all, dtype=jnp.int32)[None, None, :],
            route_weights[:, :, None],
            0.0,
        ),
        axis=1,
    )
    table_high = table.astype(jnp.bfloat16)
    table_low = (table - table_high.astype(jnp.float32)).astype(jnp.bfloat16)
    kv_width = KV_HEADS * head_dim
    small = jnp.concatenate(
        [key_rows, value_rows, jnp.pad(jnp.concatenate([table_high, table_low], axis=1), ((0, 0), (0, 128 - 2 * experts_all)))],
        axis=1,
    )
    peer = swap(small, core)
    same = swap(small, forth)
    far = swap(small, opposite)
    other = swap(peer, forth)
    line = [small, same, other, far]
    side = [swap(piece, across) for piece in line]
    line_peer = [peer] + [swap(piece, core) for j, piece in enumerate(line) if j > 0]
    side_peer = [swap(piece, core) for piece in side]
    slots = line + side + line_peer + side_peer

    half_d = width_d // 2
    columns = lax.dynamic_slice_in_dim(output_weight, part * half_d, half_d, 1)
    columns_peer = swap(columns, core)
    columns_same = swap(columns, forth)
    columns_other = swap(columns_peer, forth)
    side_columns = [swap(columns, across)]
    kept, given = attention(queries, slots, window_start, device, size, kv_width)
    got = swap(given, core)
    kept_pair = swap(kept, other_part, "grp")
    got_pair = swap(got, other_part, "grp")
    columns_far = swap(columns_same, forth)
    line_columns = [columns, columns_same, columns_other, columns_far]
    side_columns += [swap(piece, across) for piece in line_columns[1:]]
    own, pair, sent = project(kept, got, kept_pair, got_pair, line_columns + side_columns)
    own_half, sent = halves(own, pair, swap(sent, core))
    other_half = swap(sent, other_part, "grp")
    residual, normed = normalise(hidden_in, own_half, other_half, norm_gain, part)

    peer = swap(normed, core)
    first = after(normed, peer)
    same = swap(first, forth)
    other = swap(peer, forth)
    far = swap(same, forth)
    line = [normed, same, other, far]
    side = [swap(first, across)]
    side += [swap(piece, across) for piece in line[1:]]
    line_peer = [peer] + [swap(piece, core) for j, piece in enumerate(line) if j > 0]
    weights = (gate_weight[0], up_weight[0], down_weight[0], device, 2 * kv_width)
    one = expert(line + line_peer, slots[:4] + slots[8:12], *weights)
    side = side[:1] + [after(piece, one[0]) for piece in side[1:]]
    side_peer = [swap(piece, core) for piece in side]
    two = expert(side + side_peer, slots[4:8] + slots[12:], *weights)

    kind = jnp.bfloat16
    total = [None] * 4
    for j in (3, 2, 1, 0):
        there = add(two[j], swap(two[4 + j], core)).astype(kind)
        here = add(one[j], swap(one[4 + j], core))
        total[j] = here + swap(there, across).astype(jnp.float32)
    same = total[1] + swap(total[3].astype(kind), back).astype(jnp.float32)
    other = swap(swap(total[2].astype(kind), back), core)
    mixture = total[0] + other.astype(jnp.float32) + swap(same.astype(kind), back).astype(jnp.float32)
    return (residual.astype(jnp.float32) + mixture).astype(jnp.bfloat16)


def suits(size, parts, local_experts, top, rows, head_dim):
    return size * local_experts <= 2 * top and parts == 2 and size == 16 and local_experts == 1 and rows == head_dim


def on_device(*arrays):
    sizes = (arrays[9].shape[0], arrays[7].shape[1], arrays[5].shape[0], arrays[2].shape[1] // KV_HEADS)
    if suits(lax.axis_size("seq"), lax.axis_size("grp"), *sizes):
        return gathered_plan(*arrays)
    return spread_out(*arrays)


def solution(mesh):
    return jax.shard_map(
        on_device,
        mesh=mesh,
        in_specs=(
            P(("grp", "seq"), None),
            P(("grp", "seq"), None),
            P(("grp", "seq"), None),
            P(("grp", "seq"), None),
            P(("grp", "seq")),
            P("seq", None),
            P(),
            P(("grp", "seq"), None),
            P(("grp", "seq"), None),
            P("seq", None, None),
            P("seq", None, None),
            P("seq", None, None),
        ),
        out_specs=P(("grp", "seq"), None),
        check_vma=False,
    )
```
